256 devices in a mesh: ops: 16 (over x, z_lo, core), sec: 16 (over z_hi, y).
Axes of the slice: x: 4, y: 4, z: 8 (z_hi: 4, z_lo: 2; z = z_hi * 2 + z_lo), core: 2. Of those that a mesh axis runs over, the one named last changes fastest.
Arguments:
- wavefunction: float32 [16, 640, 640], P('sec'), may hold values from -6 to 6
- left_ops: bfloat16 [16, 48, 640, 640], P('sec', 'ops'), may hold values from -0.3125 to 0.3125
- right_ops: bfloat16 [16, 48, 640, 640], P('sec', 'ops'), may hold values from -0.25 to 0.25
- charge_step: int32 [16, 48], P('sec', 'ops'), may hold values from -1 to 1
- sector_sizes: int32 [16], replicated, may hold values from 320 to 640
Outputs:
- cheb_prev: float32 [16, 640, 640], P('sec', 'ops')
- cheb_last: float32 [16, 640, 640], P('sec', 'ops')
The draws below stay inside these ranges and needn't reach their ends.
Inputs may be any that keep to these rules, and one draw needn't show every extreme that they name: Operator pair p of sector t reads sector t + charge_step[t, p].
All inputs are finite; a program needn't handle non-finite values.
Results may differ from the reference program's by a relative error of at most 0.0076.
Values may be sent and summed in bfloat16 or wider, within the bound.
No kernel may reach another device: no remote copies, remote signals or barrier semaphores. Data moves between devices by JAX's collectives and lax.ppermute only.
A program may use at most 64 MiB of HBM per device.

```python
import jax
import jax.numpy as jnp
from jax import lax

W = 640
STEPS = 2
SECTORS = 16
PAIRS = 48


def place_ends(array, rng, low, largest):
    spot = [jax.random.randint(jax.random.fold_in(rng, axis), (), 0, length) for axis, length in enumerate(array.shape)]
    widest = array.shape.index(max(array.shape))
    beside = spot[:widest] + [(spot[widest] + 1) % array.shape[widest]] + spot[widest + 1:]
    return array.at[tuple(spot)].set(low).at[tuple(beside)].set(largest)


def strengthened(values, stream_key, source, target, blocks, factor):
    owner, partner = [(jnp.arange(values.shape[axis_at]) // (values.shape[axis_at] // blocks)).reshape([-1 if axis == axis_at else 1 for axis in range(values.ndim)]) for axis_at in (source, target)]
    chosen = jax.random.permutation(stream_key, blocks)[partner]
    strong = (owner == chosen) | (owner == (partner + blocks // 2) % blocks)
    return jnp.where(strong, factor * values, values)


def block_scale(stream_key, extent, pieces, smallest, high):
    level = 1.0
    for axis_at, parts in pieces:
        steps = jax.random.uniform(jax.random.fold_in(jax.random.fold_in(stream_key, 6), axis_at), (parts,), jnp.float32, smallest / len(pieces), high / len(pieces))
        level = level * jnp.repeat(jnp.exp(steps), extent[axis_at] // parts).reshape((-1,) + (1,) * (len(extent) - 1 - axis_at))
    return level


def gaussian(rng, shape, deviation, limit, pieces=(), kind=jnp.bfloat16):
    result = deviation * jax.random.normal(rng, shape, jnp.float32)
    if pieces:
        result = result * block_scale(rng, shape, pieces, -0.22, 0.18)
    return jnp.clip(result, -limit, limit).astype(kind)


def bell_draw_with(stream_key, shape, deviation, bound, pieces, heavy, kind=jnp.bfloat16):
    entries = deviation * jax.random.normal(stream_key, shape, jnp.float32)
    if pieces:
        entries = entries * block_scale(stream_key, shape, pieces, -0.22, 0.18)
    return jnp.clip(strengthened(entries, jax.random.fold_in(stream_key, 3), *heavy), -bound, bound).astype(kind)


def setup_inputs(seed: int = 0) -> dict:
    streams_of = jax.random.split(jax.random.key(seed), 6)
    return {
        "wavefunction": gaussian(streams_of[0], (SECTORS, W, W), 1.0, 6.0, ((0, 16),), jnp.float32),
        "left_ops": bell_draw_with(streams_of[1], (SECTORS, PAIRS, W, W), W ** -0.5, 0.3125, ((0, 16), (1, 16)), (1, 2, 16, 2.0)),
        "right_ops": gaussian(streams_of[2], (SECTORS, PAIRS, W, W), W ** -0.5, 0.25, ((0, 16), (1, 16))),
        "charge_step": place_ends(jax.random.randint(streams_of[3], (SECTORS, PAIRS), -1, 2), jax.random.fold_in(streams_of[3], 1), -1, 1).astype(jnp.int32),
        "sector_sizes": place_ends(jax.random.randint(streams_of[4], (SECTORS,), W // 2, W + 1), jax.random.fold_in(streams_of[4], 1), W // 2, W).astype(jnp.int32),
    }


def live_masks(sector_sizes):
    live_rows = (jnp.arange(W, dtype=jnp.int32)[None, :] < sector_sizes[:, None]).astype(jnp.float32)
    return live_rows[:, :, None] * live_rows[:, None, :]


def hamiltonian(vector, left_ops, right_ops, charge_step, live_mask):
    rounded = vector.astype(jnp.bfloat16).astype(jnp.float32)
    padded = jnp.pad(rounded, ((1, 1), (0, 0), (0, 0)))
    norm_scale = 1.0 / (PAIRS ** 0.5)

    def sector(sector_index):
        nearby = lax.dynamic_slice_in_dim(padded, sector_index, 3, 0)
        onehot = (charge_step[sector_index][:, None] + 1 == jnp.arange(3, dtype=jnp.int32)[None, :]).astype(jnp.float32)
        inputs = jnp.einsum("pc,cab->pab", onehot, nearby, precision=lax.Precision.HIGHEST)
        left_block = left_ops[sector_index].astype(jnp.float32)
        left_half = jnp.einsum("pab,pbc->pac", left_block, inputs, precision=lax.Precision.HIGHEST)
        left_half = left_half.astype(jnp.bfloat16).astype(jnp.float32)
        right_block = right_ops[sector_index].astype(jnp.float32)
        summed = jnp.einsum("pac,pdc->ad", left_half, right_block, precision=lax.Precision.HIGHEST)
        return summed * norm_scale * live_mask[sector_index]

    return lax.map(sector, jnp.arange(SECTORS, dtype=jnp.int32))


def reference(wavefunction, left_ops, right_ops, charge_step, sector_sizes):
    live_mask = live_masks(sector_sizes)
    start_field = wavefunction * live_mask
    previous = start_field
    current = hamiltonian(start_field, left_ops, right_ops, charge_step, live_mask)
    for iteration in range(1, STEPS):
        updated = 2.0 * hamiltonian(current, left_ops, right_ops, charge_step, live_mask) - previous
        previous, current = current, updated
    return previous, current
```

```python
import math

import jax
import jax.numpy as jnp
from jax import lax
from jax.experimental import pallas as pl
from jax.experimental.pallas import tpu as pltpu
from jax.sharding import PartitionSpec as P

STEPS = 2
AXES = ("ops", "sec")


def pairs(ops_count, sec_count, partner):
    found = []
    for o in range(ops_count):
        for s in range(sec_count):
            to_o, to_s = partner(o, s)
            if 0 <= to_s < sec_count:
                found.append((o * sec_count + s, to_o * sec_count + to_s))
    return found


def apply_kernel(info_ref, charge_ref, *refs):
    sources, (left_ref, right_ref, mine_ref, other_ref, field_ref, total_ref) = refs[:-6], refs[-6:]
    pair = pl.program_id(0)
    core, parity = info_ref[0], info_ref[1]

    @pl.when(pair == 0)
    def _():
        if len(sources) == 2:
            near, far = sources
            blocks = near.shape[0]
            for part, owner in ((near, core), (far, 1 - core)):
                for slot in range(3):
                    for block in range(blocks):
                        row = pl.multiple_of(80 * block + 40 * owner, 8)
                        field_ref[slot, pl.ds(row, 40), :] = part[block, slot].astype(jnp.float32)
        else:
            own, *halves = sources
            field_ref[0] = own[...].astype(jnp.float32)
            for slot in (1, 2):
                near, far = halves[2 * slot - 2], halves[2 * slot - 1]
                half = near.shape[0]
                field_ref[slot, pl.ds(pl.multiple_of(half * core, 8), half), :] = near[...].astype(jnp.float32)
                field_ref[slot, pl.ds(pl.multiple_of(half * (1 - core), 8), half), :] = far[...].astype(jnp.float32)

    charge = charge_ref[pair]
    slot = jnp.where(charge == 0, 0, jnp.where((charge > 0) == (parity == 0), 1, 2))
    source = field_ref[slot].astype(jnp.bfloat16)
    left_half = jnp.dot(left_ref[0], source, preferred_element_type=jnp.float32).astype(jnp.bfloat16)
    product = lax.dot_general(
        left_half, right_ref[0], (((1,), (1,)), ((), ())), preferred_element_type=jnp.float32
    )

    @pl.when(pair == 0)
    def _():
        total_ref[...] = product

    @pl.when(pair > 0)
    def _():
        total_ref[...] += product

    @pl.when(pair == pl.num_programs(0) - 1)
    def _():
        for block in range(mine_ref.shape[0]):
            mine_ref[block] = total_ref[pl.ds(pl.multiple_of(80 * block + 40 * core, 8), 40), :]
            other_ref[block] = total_ref[
                pl.ds(pl.multiple_of(80 * block + 40 * (1 - core), 8), 40), :
            ].astype(jnp.bfloat16)


def apply_pairs(info, charge, sources, left, right):
    count, width, _ = left.shape
    chips = width // 80
    whole = pl.BlockSpec(memory_space=pltpu.VMEM)
    scalars = pl.BlockSpec(memory_space=pltpu.SMEM)
    block = pl.BlockSpec((1, width, width), lambda p: (p, 0, 0))
    return pl.pallas_call(
        apply_kernel,
        grid=(count,),
        in_specs=[scalars, scalars] + [whole] * len(sources) + [block, block],
        out_specs=[whole, whole],
        out_shape=[
            jax.ShapeDtypeStruct((chips, 40, width), jnp.float32),
            jax.ShapeDtypeStruct((chips, 40, width), jnp.bfloat16),
        ],
        scratch_shapes=[
            pltpu.VMEM((3, width, width), jnp.float32),
            pltpu.VMEM((width, width), jnp.float32),
        ],
        compiler_params=pltpu.CompilerParams(dimension_semantics=("arbitrary",)),
        cost_estimate=pl.CostEstimate(
            flops=4 * count * width**3, bytes_accessed=4 * count * width**2, transcendentals=0
        ),
    )(info, charge, *sources, left, right)


def on_device(wavefunction, left_ops, right_ops, charge_step, sector_sizes):
    ops_count, sec_count = lax.axis_size("ops"), lax.axis_size("sec")
    chips = ops_count // 2
    width = wavefunction.shape[1]
    share = width // ops_count
    half = width // 2
    ops_at, sec_at = lax.axis_index("ops"), lax.axis_index("sec")
    core = lax.rem(ops_at, 2)
    info = jnp.stack([core, lax.rem(sec_at, 2)]).astype(jnp.int32)
    charge = charge_step[0]
    partner_core = pairs(ops_count, sec_count, lambda o, s: (o ^ 1, s))
    even = pairs(ops_count, sec_count, lambda o, s: (o, s ^ 1))
    odd = pairs(ops_count, sec_count, lambda o, s: (o, s + 1 if s % 2 else s - 1))
    same_core = [[o for o in range(ops_count) if o % 2 == c] for c in range(2)]

    def send(block, where):
        return lax.ppermute(block, AXES, where)

    def exchange(tiles):
        return lax.all_to_all(tiles, "ops", 0, 0, axis_index_groups=same_core, tiled=True)

    own_size = lax.dynamic_index_in_dim(sector_sizes, sec_at, 0, keepdims=False)
    live_cols = (jnp.arange(width, dtype=jnp.int32) < own_size).astype(jnp.float32)
    first_row = ops_at * share
    row_live = (jnp.arange(share, dtype=jnp.int32) + first_row < own_size).astype(jnp.float32)
    row_mask = row_live[:, None] * live_cols[None, :]
    norm_scale = 1.0 / math.sqrt(left_ops.shape[1] * ops_count)

    source = (wavefunction[0] * (live_cols[:, None] * live_cols[None, :])).astype(jnp.bfloat16)
    start_rows = lax.dynamic_slice_in_dim(wavefunction[0], first_row, share, 0) * row_mask

    near = lax.dynamic_slice_in_dim(source, core * half, half, 0)
    halves = []
    arrived = [send(near, even), send(near, odd)]
    for block in arrived:
        halves += [block, send(block, partner_core)]
    sources = [source] + halves

    outputs = [start_rows]
    for iteration in range(STEPS):
        mine, other = apply_pairs(info, charge, sources, left_ops[0], right_ops[0])
        chip_sum = (mine + send(other, partner_core).astype(jnp.float32)).astype(jnp.bfloat16)
        summed = exchange(chip_sum).astype(jnp.float32).sum(axis=0)
        applied = summed * norm_scale * row_mask
        updated = applied if iteration == 0 else 2.0 * applied - outputs[-2]
        outputs.append(updated)
        if iteration + 1 < STEPS:
            rows = updated.astype(jnp.bfloat16)
            three = jnp.stack([rows, send(rows, even), send(rows, odd)])
            near = exchange(jnp.broadcast_to(three[None], (chips, *three.shape)))
            sources = [near, send(near, partner_core)]
    return (outputs[-2][None], outputs[-1][None])


def solution(mesh):
    in_specs = (
        P("sec", None, None),
        P("sec", "ops", None, None),
        P("sec", "ops", None, None),
        P("sec", "ops"),
        P(),
    )
    out_specs = (P("sec", "ops", None), P("sec", "ops", None))
    return jax.shard_map(
        on_device, mesh=mesh, in_specs=in_specs, out_specs=out_specs, check_vma=False
    )
```

```python
import functools
import math

import jax
import jax.numpy as jnp
from jax import lax
from jax.experimental import pallas as pl
from jax.experimental.pallas import tpu as pltpu
from jax.sharding import PartitionSpec as P


STEPS = 2
AXES = ("ops", "sec")
VMEM = pl.BlockSpec(memory_space=pltpu.VMEM)
SMEM = pl.BlockSpec(memory_space=pltpu.SMEM)
ANY = pl.BlockSpec(memory_space=pl.ANY)
HBM = pl.BlockSpec(memory_space=pltpu.HBM)
MIB = 2**20


def swaps(ops_count, sec_count, partner):
    found = []
    for o in range(ops_count):
        for s in range(sec_count):
            to_o, to_s = partner(o, s)
            if 0 <= to_s < sec_count:
                found.append((o * sec_count + s, to_o * sec_count + to_s))
    return found


def in_hbm(array):
    return pltpu.with_memory_space_constraint(array, pltpu.HBM)


def live(size, first, rows, width):
    row = lax.broadcasted_iota(jnp.int32, (rows, width), 0) + first
    col = lax.broadcasted_iota(jnp.int32, (rows, width), 1)
    return jnp.where((row < size) & (col < size), 1.0, 0.0)


def first_kernel(sizes_ref, wave_ref, half_ref, slice_ref, half_buf, slice_buf, sizes_buf, sems):
    share, width = slice_ref.shape
    half = width // 2
    ops_at, sec_at = lax.axis_index("ops"), lax.axis_index("sec")
    half_row = pl.multiple_of(half * lax.rem(ops_at, 2), 8)
    slice_row = pl.multiple_of(half_row + share * (ops_at // 2), 8)
    copies = [
        pltpu.make_async_copy(sizes_ref, sizes_buf, sems.at[0]),
        pltpu.make_async_copy(wave_ref.at[pl.ds(slice_row, share), :], slice_buf, sems.at[1]),
        pltpu.make_async_copy(wave_ref.at[pl.ds(half_row, half), :], half_buf, sems.at[2]),
    ]
    for copy in copies:
        copy.start()
    for copy in copies[:2]:
        copy.wait()
    size = sizes_buf[sec_at]
    slice_ref[...] = (slice_buf[...] * live(size, slice_row, share, width)).astype(jnp.bfloat16)
    copies[2].wait()
    half_ref[...] = (half_buf[...] * live(size, half_row, half, width)).astype(jnp.bfloat16)


def prepare_first(sizes, wave, share):
    width = wave.shape[0]
    half = width // 2
    return pl.pallas_call(
        first_kernel,
        in_specs=[HBM, HBM],
        out_specs=[VMEM, VMEM],
        out_shape=[
            jax.ShapeDtypeStruct((half, width), jnp.bfloat16),
            jax.ShapeDtypeStruct((share, width), jnp.bfloat16),
        ],
        scratch_shapes=[
            pltpu.VMEM((half, width), jnp.float32),
            pltpu.VMEM((share, width), jnp.float32),
            pltpu.SMEM(sizes.shape, jnp.int32),
            pltpu.SemaphoreType.DMA((3,)),
        ],
        compiler_params=pltpu.CompilerParams(vmem_limit_bytes=4 * MIB),
        cost_estimate=pl.CostEstimate(flops=width**2, bytes_accessed=3 * width**2, transcendentals=0),
    )(in_hbm(sizes), in_hbm(wave))


def rest_kernel(norm_scale, sizes_ref, wave_ref, own_ref, start_ref, mask_ref):
    share, width = start_ref.shape
    size = sizes_ref[lax.axis_index("sec")]
    first = pl.multiple_of(share * lax.axis_index("ops"), 8)
    own_ref[...] = (wave_ref[...] * live(size, 0, width, width)).astype(jnp.bfloat16)
    mask = live(size, first, share, width)
    start_ref[...] = wave_ref[pl.ds(first, share), :] * mask
    mask_ref[...] = mask * norm_scale


def prepare_rest(sizes, wave, share, norm_scale):
    width = wave.shape[0]
    return pl.pallas_call(
        functools.partial(rest_kernel, norm_scale),
        in_specs=[SMEM, VMEM],
        out_specs=[VMEM] * 3,
        out_shape=[
            jax.ShapeDtypeStruct((width, width), jnp.bfloat16),
            jax.ShapeDtypeStruct((share, width), jnp.float32),
            jax.ShapeDtypeStruct((share, width), jnp.float32),
        ],
        compiler_params=pltpu.CompilerParams(vmem_limit_bytes=8 * MIB),
        cost_estimate=pl.CostEstimate(flops=width**2, bytes_accessed=6 * width**2, transcendentals=0),
    )(sizes, wave)


def apply_kernel(n_whole, charge_ref, *refs):
    wholes, (near_ref, far_ref, left_hbm, right_hbm, mine_ref, other_ref) = refs[:n_whole], refs[n_whole : n_whole + 6]
    field_ref, half_ref, total_ref, left_ref, right_ref, left_sems, right_sems, whole_sems = refs[n_whole + 6 :]
    count, width, _ = left_ref.shape
    blocks, share, _ = mine_ref.shape
    half = width // 2
    ops_at, sec_at = lax.axis_index("ops"), lax.axis_index("sec")
    core, parity = lax.rem(ops_at, 2), lax.rem(sec_at, 2)

    copies = []
    for k, ref in enumerate(wholes):
        if k == 0:
            target = field_ref.at[0]
        else:
            owner = core if k == 1 else 1 - core
            target = field_ref.at[1, pl.ds(pl.multiple_of(half * owner, 16), half), :]
        copies.append(pltpu.make_async_copy(ref, target, whole_sems.at[k]))
    lefts = [pltpu.make_async_copy(left_hbm.at[p], left_ref.at[p], left_sems.at[p]) for p in range(count)]
    rights = [pltpu.make_async_copy(right_hbm.at[p], right_ref.at[p], right_sems.at[p]) for p in range(count)]
    for copy in copies + lefts + rights:
        copy.start()

    for c in range(2):

        @pl.when(core == c)
        def _():
            for part, owner in ((near_ref, c), (far_ref, 1 - c)):
                for block in range(blocks):
                    if n_whole:
                        row = owner * half + block * share
                        field_ref[2, row : row + share, :] = part[block]
                    else:
                        row = (2 * block + owner) * share
                        for slot in range(3):
                            field_ref[slot, row : row + share, :] = part[block, slot]

    for copy in copies:
        copy.wait()
    for pair in range(count):
        charge = charge_ref[0, pair]
        slot = jnp.where(charge == 0, 0, jnp.where((charge > 0) == (parity == 0), 1, 2))
        lefts[pair].wait()
        half_ref[:, width * pair : width * (pair + 1)] = jnp.dot(
            left_ref[pair], field_ref[slot], preferred_element_type=jnp.float32
        ).astype(jnp.bfloat16)
    for copy in rights:
        copy.wait()
    total_ref[...] = sum(
        lax.dot_general(
            half_ref[:, width * pair : width * (pair + 1)],
            right_ref[pair],
            (((1,), (1,)), ((), ())),
            preferred_element_type=jnp.float32,
        )
        for pair in range(count)
    )
    for c in range(2):

        @pl.when(core == c)
        def _():
            for block in range(blocks):
                row = (2 * block + c) * share
                mine_ref[block] = total_ref[row : row + share, :]
                row = (2 * block + 1 - c) * share
                other_ref[block] = total_ref[row : row + share, :].astype(jnp.bfloat16)


def apply_pairs(charge, wholes, near, far, left, right, share):
    count, width, _ = left.shape
    blocks = width // share // 2
    return pl.pallas_call(
        functools.partial(apply_kernel, len(wholes)),
        in_specs=[SMEM] + [ANY] * len(wholes) + [VMEM, VMEM, HBM, HBM],
        out_specs=[VMEM, VMEM],
        out_shape=[
            jax.ShapeDtypeStruct((blocks, share, width), jnp.float32),
            jax.ShapeDtypeStruct((blocks, share, width), jnp.bfloat16),
        ],
        scratch_shapes=[
            pltpu.VMEM((3, width, width), jnp.bfloat16),
            pltpu.VMEM((width, count * width), jnp.bfloat16),
            pltpu.VMEM((width, width), jnp.float32),
            pltpu.VMEM((count, width, width), jnp.bfloat16),
            pltpu.VMEM((count, width, width), jnp.bfloat16),
            pltpu.SemaphoreType.DMA((count,)),
            pltpu.SemaphoreType.DMA((count,)),
            pltpu.SemaphoreType.DMA((3,)),
        ],
        compiler_params=pltpu.CompilerParams(vmem_limit_bytes=24 * MIB),
        cost_estimate=pl.CostEstimate(
            flops=4 * count * width**3, bytes_accessed=4 * count * width**2, transcendentals=0
        ),
    )(charge, *wholes, near, far, in_hbm(left), in_hbm(right))


def on_device(wavefunction, left_ops, right_ops, charge_step, sector_sizes):
    ops_count, sec_count = lax.axis_size("ops"), lax.axis_size("sec")
    chips = ops_count // 2
    width = wavefunction.shape[1]
    share = width // ops_count
    norm_scale = 1.0 / math.sqrt(left_ops.shape[1] * ops_count)
    partner_core = swaps(ops_count, sec_count, lambda o, s: (o ^ 1, s))
    even = swaps(ops_count, sec_count, lambda o, s: (o, s ^ 1))
    odd = swaps(ops_count, sec_count, lambda o, s: (o, s + 1 if s % 2 else s - 1))
    same_core = [[o for o in range(ops_count) if o % 2 == c] for c in range(2)]

    def send(block, where):
        return lax.ppermute(block, AXES, where)

    def exchange(tiles):
        return lax.all_to_all(tiles, "ops", 0, 0, axis_index_groups=same_core, tiled=True)

    def spread(rows):
        return exchange(jnp.broadcast_to(rows[None], (chips, *rows.shape)))

    half, first = prepare_first(sector_sizes, wavefunction[0], share)
    own, start_rows, scaled_mask = prepare_rest(sector_sizes, wavefunction[0], share, norm_scale)
    even_near = send(half, even)
    odd_rows = send(first, odd)
    near = spread(odd_rows)
    even_far = send(even_near, partner_core)
    far = send(near, partner_core)
    wholes = [own, even_near, even_far]

    outputs = [start_rows]
    for iteration in range(STEPS):
        mine, other = apply_pairs(charge_step, wholes, near, far, left_ops[0], right_ops[0], share)
        chip_sum = (mine + send(other, partner_core).astype(jnp.float32)).astype(jnp.bfloat16)
        applied = exchange(chip_sum).astype(jnp.float32).sum(axis=0) * scaled_mask
        updated = applied if iteration == 0 else 2.0 * applied - outputs[-2]
        outputs.append(updated)
        if iteration + 1 < STEPS:
            rows = updated.astype(jnp.bfloat16)
            even_rows = send(rows, even)
            three = jnp.stack([rows, even_rows, send(rows, odd)])
            near = spread(three)
            far = send(near, partner_core)
            wholes = []
    return (outputs[-2][None], outputs[-1][None])


def solution(mesh):
    in_specs = (
        P("sec", None, None),
        P("sec", "ops", None, None),
        P("sec", "ops", None, None),
        P("sec", "ops"),
        P(),
    )
    out_specs = (P("sec", "ops", None), P("sec", "ops", None))
    return jax.shard_map(
        on_device, mesh=mesh, in_specs=in_specs, out_specs=out_specs, check_vma=False
    )
```

```python
import functools
import math

import jax
import jax.numpy as jnp
from jax import lax
from jax.experimental import pallas as pl
from jax.experimental.pallas import tpu as pltpu
from jax.sharding import PartitionSpec as P


STEPS = 2
AXES = ("ops", "sec")
VMEM = pl.BlockSpec(memory_space=pltpu.VMEM)
SMEM = pl.BlockSpec(memory_space=pltpu.SMEM)
ANY = pl.BlockSpec(memory_space=pl.ANY)
HBM = pl.BlockSpec(memory_space=pltpu.HBM)
MIB = 2**20


def swaps(ops_count, sec_count, partner):
    found = []
    for o in range(ops_count):
        for s in range(sec_count):
            to_o, to_s = partner(o, s)
            if 0 <= to_s < sec_count:
                found.append((o * sec_count + s, to_o * sec_count + to_s))
    return found


def in_hbm(array):
    return pltpu.with_memory_space_constraint(array, pltpu.HBM)


def live(size, first, rows, width):
    row = lax.broadcasted_iota(jnp.int32, (rows, width), 0) + first
    col = lax.broadcasted_iota(jnp.int32, (rows, width), 1)
    return jnp.where((row < size) & (col < size), 1.0, 0.0)


def cut_kernel(first_row, sizes_ref, wave_ref, out_ref, wave_buf, sizes_buf, sems):
    rows, width = out_ref.shape
    first = pl.multiple_of(first_row(lax.axis_index("ops")), 8)
    copies = [
        pltpu.make_async_copy(sizes_ref, sizes_buf, sems.at[0]),
        pltpu.make_async_copy(wave_ref.at[pl.ds(first, rows), :], wave_buf, sems.at[1]),
    ]
    for copy in copies:
        copy.start()
    for copy in copies:
        copy.wait()
    size = sizes_buf[lax.axis_index("sec")]
    out_ref[...] = (wave_buf[...] * live(size, first, rows, width)).astype(jnp.bfloat16)


def masked_rows(sizes, wave, rows, first_row):
    width = wave.shape[0]
    return pl.pallas_call(
        functools.partial(cut_kernel, first_row),
        in_specs=[HBM, HBM],
        out_specs=VMEM,
        out_shape=jax.ShapeDtypeStruct((rows, width), jnp.bfloat16),
        scratch_shapes=[
            pltpu.VMEM((rows, width), jnp.float32),
            pltpu.SMEM(sizes.shape, jnp.int32),
            pltpu.SemaphoreType.DMA((2,)),
        ],
        compiler_params=pltpu.CompilerParams(vmem_limit_bytes=4 * MIB),
        cost_estimate=pl.CostEstimate(flops=rows * width, bytes_accessed=6 * rows * width, transcendentals=0),
    )(in_hbm(sizes), in_hbm(wave))


def rest_kernel(norm_scale, sizes_ref, wave_ref, left_hbm, own_hbm, start_ref, mask_ref, left_ref, own_buf, sizes_buf, sems, own_sem, sizes_sem):
    share, width = start_ref.shape
    count, owners, blocks = left_ref.shape[0], 2, width // share // 2
    copies = []
    for pair in range(count):
        for owner in range(owners):
            for block in range(blocks):
                copies.append(
                    pltpu.make_async_copy(
                        left_hbm.at[pair, pl.ds((2 * block + owner) * share, share), :],
                        left_ref.at[pair, pl.ds((owner * blocks + block) * share, share), :],
                        sems.at[(pair * owners + owner) * blocks + block],
                    )
                )
    sizes_copy = pltpu.make_async_copy(sizes_ref, sizes_buf, sizes_sem)
    for copy in [sizes_copy] + copies:
        copy.start()
    sizes_copy.wait()
    size = sizes_buf[lax.axis_index("sec")]
    first = pl.multiple_of(share * lax.axis_index("ops"), 8)
    own_buf[...] = (wave_ref[...] * live(size, 0, width, width)).astype(jnp.bfloat16)
    own_copy = pltpu.make_async_copy(own_buf, own_hbm, own_sem)
    own_copy.start()
    mask = live(size, first, share, width)
    start_ref[...] = wave_ref[pl.ds(first, share), :] * mask
    mask_ref[...] = mask * norm_scale
    for copy in copies + [own_copy]:
        copy.wait()


def prepare_rest(sizes, wave, left, share, norm_scale):
    width = wave.shape[0]
    return pl.pallas_call(
        functools.partial(rest_kernel, norm_scale),
        in_specs=[HBM, VMEM, HBM],
        out_specs=[HBM] + [VMEM] * 3,
        out_shape=[
            pltpu.HBM((width, width), jnp.bfloat16),
            jax.ShapeDtypeStruct((share, width), jnp.float32),
            jax.ShapeDtypeStruct((share, width), jnp.float32),
            jax.ShapeDtypeStruct(left.shape, left.dtype),
        ],
        scratch_shapes=[
            pltpu.VMEM((width, width), jnp.bfloat16),
            pltpu.SMEM(sizes.shape, jnp.int32),
            pltpu.SemaphoreType.DMA((left.shape[0] * width // share,)),
            pltpu.SemaphoreType.DMA,
            pltpu.SemaphoreType.DMA,
        ],
        compiler_params=pltpu.CompilerParams(vmem_limit_bytes=12 * MIB),
        cost_estimate=pl.CostEstimate(flops=width**2, bytes_accessed=18 * width**2, transcendentals=0),
    )(in_hbm(sizes), wave, in_hbm(left))


def products(charge_ref, field_ref, left_ref, right_ref, half_ref, owner, before_right):
    count, width, _ = left_ref.shape
    rows = width // 2
    parity = lax.rem(lax.axis_index("sec"), 2)
    first = pl.multiple_of(rows * owner, 16)
    for pair in range(count):
        charge = charge_ref[0, pair]
        slot = jnp.where(charge == 0, 0, jnp.where((charge > 0) == (parity == 0), 1, 2))
        half_ref[:, width * pair : width * (pair + 1)] = jnp.dot(
            left_ref[pair, pl.ds(first, rows), :], field_ref[slot], preferred_element_type=jnp.float32
        ).astype(jnp.bfloat16)
    before_right()
    return sum(
        lax.dot_general(
            half_ref[:, width * pair : width * (pair + 1)],
            right_ref[pair],
            (((1,), (1,)), ((), ())),
            preferred_element_type=jnp.float32,
        )
        for pair in range(count)
    )


def other_kernel(n_whole, charge_ref, *refs):
    wholes, (near_ref, far_ref, left_ref, right_hbm, other_ref, field_ref, right_ref) = refs[:n_whole], refs[n_whole : n_whole + 7]
    half_ref, right_sem, whole_sems = refs[n_whole + 7 :]
    width = field_ref.shape[1]
    half = width // 2
    core = lax.rem(lax.axis_index("ops"), 2)

    copies = []
    for k, ref in enumerate(wholes):
        if k == 0:
            target = field_ref.at[0]
        else:
            owner = core if k == 1 else 1 - core
            target = field_ref.at[1, pl.ds(pl.multiple_of(half * owner, 16), half), :]
        copies.append(pltpu.make_async_copy(ref, target, whole_sems.at[k]))
    right_copy = pltpu.make_async_copy(right_hbm, right_ref, right_sem)
    for copy in copies or [right_copy]:
        copy.start()

    blocks = near_ref.shape[0]
    share = half // blocks
    for c in range(2):

        @pl.when(core == c)
        def _():
            for part, owner in ((near_ref, c), (far_ref, 1 - c)):
                for block in range(blocks):
                    if n_whole:
                        row = owner * half + block * share
                        field_ref[2, row : row + share, :] = part[block]
                    else:
                        row = (2 * block + owner) * share
                        for slot in range(3):
                            field_ref[slot, row : row + share, :] = part[block, slot]

    for copy in copies:
        copy.wait()
    if copies:
        right_copy.start()
    other_ref[...] = products(
        charge_ref, field_ref, left_ref, right_ref, half_ref, 1 - core, right_copy.wait
    ).astype(jnp.bfloat16)


def mine_kernel(charge_ref, field_ref, left_ref, right_ref, mine_ref, half_ref):
    core = lax.rem(lax.axis_index("ops"), 2)
    mine_ref[...] = products(charge_ref, field_ref, left_ref, right_ref, half_ref, core, lambda: None)


def cost(count, width):
    return pl.CostEstimate(flops=2 * count * width**3, bytes_accessed=4 * count * width**2, transcendentals=0)


def other_rows(charge, wholes, near, far, left, right):
    count, width, _ = left.shape
    return pl.pallas_call(
        functools.partial(other_kernel, len(wholes)),
        in_specs=[SMEM] + [ANY] * len(wholes) + [VMEM, VMEM, VMEM, HBM],
        out_specs=[VMEM] * 3,
        out_shape=[
            jax.ShapeDtypeStruct((width // 2, width), jnp.bfloat16),
            jax.ShapeDtypeStruct((3, width, width), jnp.bfloat16),
            jax.ShapeDtypeStruct(right.shape, right.dtype),
        ],
        scratch_shapes=[
            pltpu.VMEM((width // 2, count * width), jnp.bfloat16),
            pltpu.SemaphoreType.DMA,
            pltpu.SemaphoreType.DMA((3,)),
        ],
        compiler_params=pltpu.CompilerParams(vmem_limit_bytes=20 * MIB),
        cost_estimate=cost(count, width),
    )(charge, *wholes, near, far, left, in_hbm(right))


def mine_rows(charge, field, left, right):
    count, width, _ = left.shape
    return pl.pallas_call(
        mine_kernel,
        in_specs=[SMEM, VMEM, VMEM, VMEM],
        out_specs=VMEM,
        out_shape=jax.ShapeDtypeStruct((width // 2, width), jnp.float32),
        scratch_shapes=[pltpu.VMEM((width // 2, count * width), jnp.bfloat16)],
        compiler_params=pltpu.CompilerParams(vmem_limit_bytes=16 * MIB),
        cost_estimate=cost(count, width),
    )(charge, field, left, right)


def on_device(wavefunction, left_ops, right_ops, charge_step, sector_sizes):
    ops_count, sec_count = lax.axis_size("ops"), lax.axis_size("sec")
    chips = ops_count // 2
    width = wavefunction.shape[1]
    share = width // ops_count
    norm_scale = 1.0 / math.sqrt(left_ops.shape[1] * ops_count)
    partner_core = swaps(ops_count, sec_count, lambda o, s: (o ^ 1, s))
    even = swaps(ops_count, sec_count, lambda o, s: (o, s ^ 1))
    odd = swaps(ops_count, sec_count, lambda o, s: (o, s + 1 if s % 2 else s - 1))
    same_core = [[o for o in range(ops_count) if o % 2 == c] for c in range(2)]

    def send(block, where):
        return lax.ppermute(block, AXES, where)

    def exchange(tiles):
        return lax.all_to_all(tiles, "ops", 0, 0, axis_index_groups=same_core, tiled=True)

    def spread(rows):
        return exchange(jnp.broadcast_to(rows[None], (chips, *rows.shape)))

    wave = wavefunction[0]
    half = width // 2
    first = masked_rows(sector_sizes, wave, share, lambda o: half * lax.rem(o, 2) + share * (o // 2))
    odd_rows = send(first, odd)
    block = masked_rows(sector_sizes, wave, half, lambda o: half * lax.rem(o, 2))
    even_near = send(block, even)
    own, start_rows, scaled_mask, left = prepare_rest(
        sector_sizes, wave, left_ops[0], share, norm_scale
    )
    near = spread(odd_rows)
    near, even_near = lax.optimization_barrier((near, even_near))
    even_far = send(even_near, partner_core)
    far = send(near, partner_core)
    wholes = [in_hbm(own), even_near, even_far]

    outputs = [start_rows]
    for iteration in range(STEPS):
        other, field, right = other_rows(charge_step, wholes, near, far, left, right_ops[0])
        partner_sum = send(other, partner_core)
        mine = mine_rows(charge_step, field, left, right)
        chip_sum = (mine + partner_sum.astype(jnp.float32)).astype(jnp.bfloat16)
        applied = exchange(chip_sum.reshape(chips, share, width)).astype(jnp.float32).sum(axis=0) * scaled_mask
        updated = applied if iteration == 0 else 2.0 * applied - outputs[-2]
        outputs.append(updated)
        if iteration + 1 < STEPS:
            rows = updated.astype(jnp.bfloat16)
            even_rows = send(rows, even)
            three = jnp.stack([rows, even_rows, send(rows, odd)])
            near = spread(three)
            far = send(near, partner_core)
            wholes = []
    return (outputs[-2][None], outputs[-1][None])


def solution(mesh):
    in_specs = (
        P("sec", None, None),
        P("sec", "ops", None, None),
        P("sec", "ops", None, None),
        P("sec", "ops"),
        P(),
    )
    out_specs = (P("sec", "ops", None), P("sec", "ops", None))
    return jax.shard_map(
        on_device, mesh=mesh, in_specs=in_specs, out_specs=out_specs, check_vma=False
    )
```

```python
import functools
import math

import jax
import jax.numpy as jnp
from jax import lax
from jax.experimental import pallas as pl
from jax.experimental.pallas import tpu as pltpu
from jax.sharding import PartitionSpec as P


STEPS = 2
AXES = ("ops", "sec")
VMEM = pl.BlockSpec(memory_space=pltpu.VMEM)
SMEM = pl.BlockSpec(memory_space=pltpu.SMEM)
HBM = pl.BlockSpec(memory_space=pltpu.HBM)
MIB = 2**20


def swaps(ops_count, sec_count, partner):
    found = []
    for o in range(ops_count):
        for s in range(sec_count):
            to_o, to_s = partner(o, s)
            if 0 <= to_s < sec_count:
                found.append((o * sec_count + s, to_o * sec_count + to_s))
    return found


def in_hbm(array):
    return pltpu.with_memory_space_constraint(array, pltpu.HBM)


def live(size, first, rows, width):
    row = lax.broadcasted_iota(jnp.int32, (rows, width), 0) + first
    col = lax.broadcasted_iota(jnp.int32, (rows, width), 1)
    return jnp.where((row < size) & (col < size), 1.0, 0.0)


def cut_kernel(first_row, sizes_ref, wave_ref, out_ref, wave_buf, sizes_buf, sems):
    rows, width = out_ref.shape
    first = pl.multiple_of(first_row(lax.axis_index("ops")), 8)
    copies = [
        pltpu.make_async_copy(sizes_ref, sizes_buf, sems.at[0]),
        pltpu.make_async_copy(wave_ref.at[pl.ds(first, rows), :], wave_buf, sems.at[1]),
    ]
    for copy in copies:
        copy.start()
    for copy in copies:
        copy.wait()
    size = sizes_buf[lax.axis_index("sec")]
    out_ref[...] = (wave_buf[...] * live(size, first, rows, width)).astype(jnp.bfloat16)


def masked_rows(sizes, wave, rows, first_row):
    width = wave.shape[0]
    return pl.pallas_call(
        functools.partial(cut_kernel, first_row),
        in_specs=[HBM, HBM],
        out_specs=VMEM,
        out_shape=jax.ShapeDtypeStruct((rows, width), jnp.bfloat16),
        scratch_shapes=[
            pltpu.VMEM((rows, width), jnp.float32),
            pltpu.SMEM(sizes.shape, jnp.int32),
            pltpu.SemaphoreType.DMA((2,)),
        ],
        compiler_params=pltpu.CompilerParams(vmem_limit_bytes=4 * MIB),
        cost_estimate=pl.CostEstimate(flops=rows * width, bytes_accessed=6 * rows * width, transcendentals=0),
    )(in_hbm(sizes), in_hbm(wave))


def rest_kernel(norm_scale, sizes_ref, wave_ref, left_hbm, own_ref, start_ref, mask_ref, left_ref, sizes_buf, sems, sizes_sem):
    share, width = start_ref.shape
    count, owners, blocks = left_ref.shape[0], 2, width // share // 2
    copies = []
    for pair in range(count):
        for owner in range(owners):
            for block in range(blocks):
                copies.append(
                    pltpu.make_async_copy(
                        left_hbm.at[pair, pl.ds((2 * block + owner) * share, share), :],
                        left_ref.at[pair, pl.ds((owner * blocks + block) * share, share), :],
                        sems.at[(pair * owners + owner) * blocks + block],
                    )
                )
    sizes_copy = pltpu.make_async_copy(sizes_ref, sizes_buf, sizes_sem)
    for copy in [sizes_copy] + copies:
        copy.start()
    sizes_copy.wait()
    size = sizes_buf[lax.axis_index("sec")]
    first = pl.multiple_of(share * lax.axis_index("ops"), 8)
    own_ref[...] = (wave_ref[...] * live(size, 0, width, width)).astype(jnp.bfloat16)
    mask = live(size, first, share, width)
    start_ref[...] = wave_ref[pl.ds(first, share), :] * mask
    mask_ref[...] = mask * norm_scale
    for copy in copies:
        copy.wait()


def prepare_rest(sizes, wave, left, share, norm_scale):
    width = wave.shape[0]
    return pl.pallas_call(
        functools.partial(rest_kernel, norm_scale),
        in_specs=[HBM, VMEM, HBM],
        out_specs=[VMEM] * 4,
        out_shape=[
            jax.ShapeDtypeStruct((width, width), jnp.bfloat16),
            jax.ShapeDtypeStruct((share, width), jnp.float32),
            jax.ShapeDtypeStruct((share, width), jnp.float32),
            jax.ShapeDtypeStruct(left.shape, left.dtype),
        ],
        scratch_shapes=[
            pltpu.SMEM(sizes.shape, jnp.int32),
            pltpu.SemaphoreType.DMA((left.shape[0] * width // share,)),
            pltpu.SemaphoreType.DMA,
        ],
        compiler_params=pltpu.CompilerParams(vmem_limit_bytes=12 * MIB),
        cost_estimate=pl.CostEstimate(flops=width**2, bytes_accessed=18 * width**2, transcendentals=0),
    )(in_hbm(sizes), wave, in_hbm(left))


def products(charge_ref, field_ref, left_ref, right_ref, half_ref, owner, before_right):
    count, width, _ = left_ref.shape
    rows = width // 2
    parity = lax.rem(lax.axis_index("sec"), 2)
    first = pl.multiple_of(rows * owner, 16)
    for pair in range(count):
        charge = charge_ref[0, pair]
        slot = jnp.where(charge == 0, 0, jnp.where((charge > 0) == (parity == 0), 1, 2))
        half_ref[:, width * pair : width * (pair + 1)] = jnp.dot(
            left_ref[pair, pl.ds(first, rows), :], field_ref[slot], preferred_element_type=jnp.float32
        ).astype(jnp.bfloat16)
    before_right()
    return sum(
        lax.dot_general(
            half_ref[:, width * pair : width * (pair + 1)],
            right_ref[pair],
            (((1,), (1,)), ((), ())),
            preferred_element_type=jnp.float32,
        )
        for pair in range(count)
    )


def other_kernel(n_whole, charge_ref, *refs):
    wholes, (near_ref, far_ref, left_ref, right_hbm, other_ref, field_ref, right_ref) = refs[:n_whole], refs[n_whole : n_whole + 7]
    half_ref, right_sem = refs[n_whole + 7 :]
    width = field_ref.shape[1]
    half = width // 2
    core = lax.rem(lax.axis_index("ops"), 2)

    right_copy = pltpu.make_async_copy(right_hbm, right_ref, right_sem)
    right_copy.start()
    blocks = near_ref.shape[0]
    share = half // blocks
    for c in range(2):

        @pl.when(core == c)
        def _():
            if n_whole:
                field_ref[0] = wholes[0][...]
                field_ref[1, half * c : half * (c + 1), :] = wholes[1][...]
                field_ref[1, half * (1 - c) : half * (2 - c), :] = wholes[2][...]
            for part, owner in ((near_ref, c), (far_ref, 1 - c)):
                for block in range(blocks):
                    if n_whole:
                        row = owner * half + block * share
                        field_ref[2, row : row + share, :] = part[block]
                    else:
                        row = (2 * block + owner) * share
                        for slot in range(3):
                            field_ref[slot, row : row + share, :] = part[block, slot]

    other_ref[...] = products(
        charge_ref, field_ref, left_ref, right_ref, half_ref, 1 - core, right_copy.wait
    ).astype(jnp.bfloat16)


def mine_kernel(charge_ref, field_ref, left_ref, right_ref, mine_ref, half_ref):
    core = lax.rem(lax.axis_index("ops"), 2)
    mine_ref[...] = products(charge_ref, field_ref, left_ref, right_ref, half_ref, core, lambda: None)


def cost(count, width):
    return pl.CostEstimate(flops=2 * count * width**3, bytes_accessed=4 * count * width**2, transcendentals=0)


def other_rows(charge, wholes, near, far, left, right):
    count, width, _ = left.shape
    return pl.pallas_call(
        functools.partial(other_kernel, len(wholes)),
        in_specs=[SMEM] + [VMEM] * len(wholes) + [VMEM, VMEM, VMEM, HBM],
        out_specs=[VMEM] * 3,
        out_shape=[
            jax.ShapeDtypeStruct((width // 2, width), jnp.bfloat16),
            jax.ShapeDtypeStruct((3, width, width), jnp.bfloat16),
            jax.ShapeDtypeStruct(right.shape, right.dtype),
        ],
        scratch_shapes=[
            pltpu.VMEM((width // 2, count * width), jnp.bfloat16),
            pltpu.SemaphoreType.DMA,
        ],
        compiler_params=pltpu.CompilerParams(vmem_limit_bytes=20 * MIB),
        cost_estimate=cost(count, width),
    )(charge, *wholes, near, far, left, in_hbm(right))


def mine_rows(charge, field, left, right):
    count, width, _ = left.shape
    return pl.pallas_call(
        mine_kernel,
        in_specs=[SMEM, VMEM, VMEM, VMEM],
        out_specs=VMEM,
        out_shape=jax.ShapeDtypeStruct((width // 2, width), jnp.float32),
        scratch_shapes=[pltpu.VMEM((width // 2, count * width), jnp.bfloat16)],
        compiler_params=pltpu.CompilerParams(vmem_limit_bytes=16 * MIB),
        cost_estimate=cost(count, width),
    )(charge, field, left, right)


def on_device(wavefunction, left_ops, right_ops, charge_step, sector_sizes):
    ops_count, sec_count = lax.axis_size("ops"), lax.axis_size("sec")
    chips = ops_count // 2
    width = wavefunction.shape[1]
    share = width // ops_count
    norm_scale = 1.0 / math.sqrt(left_ops.shape[1] * ops_count)
    partner_core = swaps(ops_count, sec_count, lambda o, s: (o ^ 1, s))
    even = swaps(ops_count, sec_count, lambda o, s: (o, s ^ 1))
    odd = swaps(ops_count, sec_count, lambda o, s: (o, s + 1 if s % 2 else s - 1))
    same_core = [[o for o in range(ops_count) if o % 2 == c] for c in range(2)]

    def send(block, where):
        return lax.ppermute(block, AXES, where)

    def exchange(tiles):
        return lax.all_to_all(tiles, "ops", 0, 0, axis_index_groups=same_core, tiled=True)

    def spread(rows):
        return exchange(jnp.broadcast_to(rows[None], (chips, *rows.shape)))

    wave = wavefunction[0]
    half = width // 2
    first = masked_rows(sector_sizes, wave, share, lambda o: half * lax.rem(o, 2) + share * (o // 2))
    odd_rows = send(first, odd)
    block = masked_rows(sector_sizes, wave, half, lambda o: half * lax.rem(o, 2))
    even_near = send(block, even)
    own, start_rows, scaled_mask, left = prepare_rest(
        sector_sizes, wave, left_ops[0], share, norm_scale
    )
    near = spread(odd_rows)
    gate = near[0, :8, :128].astype(jnp.float32)
    even_far = send(even_near, partner_core)
    far = send(near, partner_core)
    wholes = [own, even_near, even_far, gate]

    outputs = [start_rows]
    for iteration in range(STEPS):
        other, field, right = other_rows(charge_step, wholes, near, far, left, right_ops[0])
        partner_sum = send(other, partner_core)
        mine = mine_rows(charge_step, field, left, right)
        chip_sum = (mine + partner_sum.astype(jnp.float32)).astype(jnp.bfloat16)
        applied = exchange(chip_sum.reshape(chips, share, width)).astype(jnp.float32).sum(axis=0) * scaled_mask
        updated = applied if iteration == 0 else 2.0 * applied - outputs[-2]
        outputs.append(updated)
        if iteration + 1 < STEPS:
            rows = updated.astype(jnp.bfloat16)
            even_rows = send(rows, even)
            three = jnp.stack([rows, even_rows, send(rows, odd)])
            near = spread(three)
            far = send(near, partner_core)
            wholes = []
    return (outputs[-2][None], outputs[-1][None])


def solution(mesh):
    in_specs = (
        P("sec", None, None),
        P("sec", "ops", None, None),
        P("sec", "ops", None, None),
        P("sec", "ops"),
        P(),
    )
    out_specs = (P("sec", "ops", None), P("sec", "ops", None))
    return jax.shard_map(
        on_device, mesh=mesh, in_specs=in_specs, out_specs=out_specs, check_vma=False
    )
```

```python
import functools
import math

import jax
import jax.numpy as jnp
from jax import lax
from jax.experimental import pallas as pl
from jax.experimental.pallas import tpu as pltpu
from jax.sharding import PartitionSpec as P


STEPS = 2
AXES = ("ops", "sec")
VMEM = pl.BlockSpec(memory_space=pltpu.VMEM)
SMEM = pl.BlockSpec(memory_space=pltpu.SMEM)
HBM = pl.BlockSpec(memory_space=pltpu.HBM)
MIB = 2**20
CHIP_ORDER = (0, 1, 3, 2, 4, 5, 7, 6)


def swaps(ops_count, sec_count, partner):
    found = []
    for o in range(ops_count):
        for s in range(sec_count):
            to_o, to_s = partner(o, s)
            if 0 <= to_s < sec_count:
                found.append((o * sec_count + s, to_o * sec_count + to_s))
    return found


def in_hbm(array):
    return pltpu.with_memory_space_constraint(array, pltpu.HBM)


def live(size, first, rows, width):
    row = lax.broadcasted_iota(jnp.int32, (rows, width), 0) + first
    col = lax.broadcasted_iota(jnp.int32, (rows, width), 1)
    return jnp.where((row < size) & (col < size), 1.0, 0.0)


def cut_kernel(first_row, sizes_ref, wave_ref, out_ref, wave_buf, sizes_buf, sems):
    rows, width = out_ref.shape
    first = pl.multiple_of(first_row(lax.axis_index("ops")), 8)
    copies = [
        pltpu.make_async_copy(sizes_ref, sizes_buf, sems.at[0]),
        pltpu.make_async_copy(wave_ref.at[pl.ds(first, rows), :], wave_buf, sems.at[1]),
    ]
    for copy in copies:
        copy.start()
    for copy in copies:
        copy.wait()
    size = sizes_buf[lax.axis_index("sec")]
    out_ref[...] = (wave_buf[...] * live(size, first, rows, width)).astype(jnp.bfloat16)


def masked_rows(sizes, wave, rows, first_row):
    width = wave.shape[0]
    return pl.pallas_call(
        functools.partial(cut_kernel, first_row),
        in_specs=[HBM, HBM],
        out_specs=VMEM,
        out_shape=jax.ShapeDtypeStruct((rows, width), jnp.bfloat16),
        scratch_shapes=[
            pltpu.VMEM((rows, width), jnp.float32),
            pltpu.SMEM(sizes.shape, jnp.int32),
            pltpu.SemaphoreType.DMA((2,)),
        ],
        compiler_params=pltpu.CompilerParams(vmem_limit_bytes=4 * MIB),
        cost_estimate=pl.CostEstimate(flops=rows * width, bytes_accessed=6 * rows * width, transcendentals=0),
    )(in_hbm(sizes), in_hbm(wave))


def rest_kernel(norm_scale, sizes_ref, wave_ref, left_hbm, own_ref, start_ref, mask_ref, left_ref, sizes_buf, sems, sizes_sem):
    share, width = start_ref.shape
    count, owners, blocks = left_ref.shape[0], 2, width // share // 2
    copies = []
    for pair in range(count):
        for owner in range(owners):
            for block in range(blocks):
                copies.append(
                    pltpu.make_async_copy(
                        left_hbm.at[pair, pl.ds((2 * CHIP_ORDER[block] + owner) * share, share), :],
                        left_ref.at[pair, pl.ds((owner * blocks + block) * share, share), :],
                        sems.at[(pair * owners + owner) * blocks + block],
                    )
                )
    sizes_copy = pltpu.make_async_copy(sizes_ref, sizes_buf, sizes_sem)
    for copy in [sizes_copy] + copies:
        copy.start()
    sizes_copy.wait()
    size = sizes_buf[lax.axis_index("sec")]
    first = pl.multiple_of(share * lax.axis_index("ops"), 8)
    own_ref[...] = (wave_ref[...] * live(size, 0, width, width)).astype(jnp.bfloat16)
    mask = live(size, first, share, width)
    start_ref[...] = wave_ref[pl.ds(first, share), :] * mask
    mask_ref[...] = mask * norm_scale
    for copy in copies:
        copy.wait()


def prepare_rest(sizes, wave, left, share, norm_scale):
    width = wave.shape[0]
    return pl.pallas_call(
        functools.partial(rest_kernel, norm_scale),
        in_specs=[HBM, VMEM, HBM],
        out_specs=[VMEM] * 4,
        out_shape=[
            jax.ShapeDtypeStruct((width, width), jnp.bfloat16),
            jax.ShapeDtypeStruct((share, width), jnp.float32),
            jax.ShapeDtypeStruct((share, width), jnp.float32),
            jax.ShapeDtypeStruct(left.shape, left.dtype),
        ],
        scratch_shapes=[
            pltpu.SMEM(sizes.shape, jnp.int32),
            pltpu.SemaphoreType.DMA((left.shape[0] * width // share,)),
            pltpu.SemaphoreType.DMA,
        ],
        compiler_params=pltpu.CompilerParams(vmem_limit_bytes=12 * MIB),
        cost_estimate=pl.CostEstimate(flops=width**2, bytes_accessed=18 * width**2, transcendentals=0),
    )(in_hbm(sizes), wave, in_hbm(left))


def products(charge_ref, field_ref, left_ref, right_ref, half_ref, owner, before_right):
    count, width, _ = left_ref.shape
    rows = width // 2
    parity = lax.rem(lax.axis_index("sec"), 2)
    first = pl.multiple_of(rows * owner, 16)
    for pair in range(count):
        charge = charge_ref[0, pair]
        slot = jnp.where(charge == 0, 0, jnp.where((charge > 0) == (parity == 0), 1, 2))
        half_ref[:, width * pair : width * (pair + 1)] = jnp.dot(
            left_ref[pair, pl.ds(first, rows), :], field_ref[slot], preferred_element_type=jnp.float32
        ).astype(jnp.bfloat16)
    before_right()
    return sum(
        lax.dot_general(
            half_ref[:, width * pair : width * (pair + 1)],
            right_ref[pair],
            (((1,), (1,)), ((), ())),
            preferred_element_type=jnp.float32,
        )
        for pair in range(count)
    )


def other_kernel(n_whole, charge_ref, *refs):
    wholes, (near_ref, far_ref, left_ref, right_hbm, other_ref, field_ref, right_ref) = refs[:n_whole], refs[n_whole : n_whole + 7]
    half_ref, right_sem = refs[n_whole + 7 :]
    width = field_ref.shape[1]
    half = width // 2
    core = lax.rem(lax.axis_index("ops"), 2)

    right_copy = pltpu.make_async_copy(right_hbm, right_ref, right_sem)
    right_copy.start()
    blocks = near_ref.shape[0]
    share = half // blocks
    for c in range(2):

        @pl.when(core == c)
        def _():
            if n_whole:
                field_ref[0] = wholes[0][...]
                field_ref[1, half * c : half * (c + 1), :] = wholes[1][...]
                field_ref[1, half * (1 - c) : half * (2 - c), :] = wholes[2][...]
            for part, owner in ((near_ref, c), (far_ref, 1 - c)):
                for block in range(blocks):
                    if n_whole:
                        row = owner * half + CHIP_ORDER[block] * share
                        field_ref[2, row : row + share, :] = part[block]
                    else:
                        row = (2 * CHIP_ORDER[block] + owner) * share
                        for slot in range(3):
                            field_ref[slot, row : row + share, :] = part[block, slot]

    other_ref[...] = products(
        charge_ref, field_ref, left_ref, right_ref, half_ref, 1 - core, right_copy.wait
    ).astype(jnp.bfloat16)


def mine_kernel(charge_ref, field_ref, left_ref, right_ref, mine_ref, half_ref):
    core = lax.rem(lax.axis_index("ops"), 2)
    mine_ref[...] = products(charge_ref, field_ref, left_ref, right_ref, half_ref, core, lambda: None)


def cost(count, width):
    return pl.CostEstimate(flops=2 * count * width**3, bytes_accessed=4 * count * width**2, transcendentals=0)


def other_rows(charge, wholes, near, far, left, right):
    count, width, _ = left.shape
    return pl.pallas_call(
        functools.partial(other_kernel, len(wholes)),
        in_specs=[SMEM] + [VMEM] * len(wholes) + [VMEM, VMEM, VMEM, HBM],
        out_specs=[VMEM] * 3,
        out_shape=[
            jax.ShapeDtypeStruct((width // 2, width), jnp.bfloat16),
            jax.ShapeDtypeStruct((3, width, width), jnp.bfloat16),
            jax.ShapeDtypeStruct(right.shape, right.dtype),
        ],
        scratch_shapes=[
            pltpu.VMEM((width // 2, count * width), jnp.bfloat16),
            pltpu.SemaphoreType.DMA,
        ],
        compiler_params=pltpu.CompilerParams(vmem_limit_bytes=20 * MIB),
        cost_estimate=cost(count, width),
    )(charge, *wholes, near, far, left, in_hbm(right))


def mine_rows(charge, field, left, right):
    count, width, _ = left.shape
    return pl.pallas_call(
        mine_kernel,
        in_specs=[SMEM, VMEM, VMEM, VMEM],
        out_specs=VMEM,
        out_shape=jax.ShapeDtypeStruct((width // 2, width), jnp.float32),
        scratch_shapes=[pltpu.VMEM((width // 2, count * width), jnp.bfloat16)],
        compiler_params=pltpu.CompilerParams(vmem_limit_bytes=16 * MIB),
        cost_estimate=cost(count, width),
    )(charge, field, left, right)


def on_device(wavefunction, left_ops, right_ops, charge_step, sector_sizes):
    ops_count, sec_count = lax.axis_size("ops"), lax.axis_size("sec")
    chips = ops_count // 2
    width = wavefunction.shape[1]
    share = width // ops_count
    norm_scale = 1.0 / math.sqrt(left_ops.shape[1] * ops_count)
    partner_core = swaps(ops_count, sec_count, lambda o, s: (o ^ 1, s))
    even = swaps(ops_count, sec_count, lambda o, s: (o, s ^ 1))
    odd = swaps(ops_count, sec_count, lambda o, s: (o, s + 1 if s % 2 else s - 1))
    same_core = [[2 * chip + c for chip in CHIP_ORDER] for c in range(2)]

    def send(block, where):
        return lax.ppermute(block, AXES, where)

    def exchange(tiles):
        return lax.all_to_all(tiles, "ops", 0, 0, axis_index_groups=same_core, tiled=True)

    def spread(rows):
        return exchange(jnp.broadcast_to(rows[None], (chips, *rows.shape)))

    wave = wavefunction[0]
    half = width // 2
    first = masked_rows(sector_sizes, wave, share, lambda o: half * lax.rem(o, 2) + share * (o // 2))
    odd_rows = send(first, odd)
    block = masked_rows(sector_sizes, wave, half, lambda o: half * lax.rem(o, 2))
    even_near = send(block, even)
    own, start_rows, scaled_mask, left = prepare_rest(
        sector_sizes, wave, left_ops[0], share, norm_scale
    )
    near = spread(odd_rows)
    gate = near[0, :8, :128].astype(jnp.float32)
    even_far = send(even_near, partner_core)
    far = send(near, partner_core)
    wholes = [own, even_near, even_far, gate]

    outputs = [start_rows]
    for iteration in range(STEPS):
        other, field, right = other_rows(charge_step, wholes, near, far, left, right_ops[0])
        partner_sum = send(other, partner_core)
        mine = mine_rows(charge_step, field, left, right)
        chip_sum = (mine + partner_sum.astype(jnp.float32)).astype(jnp.bfloat16)
        summed = exchange(chip_sum.reshape(chips, share, width)).astype(jnp.float32).sum(axis=0)

        def updated(total):
            applied = total * scaled_mask
            return applied if iteration == 0 else 2.0 * applied - outputs[iteration - 1]

        if iteration + 1 < STEPS:
            rows = updated(summed).astype(jnp.bfloat16)
            even_rows, odd_rows = send(rows, even), send(rows, odd)
            later, odd_rows = lax.optimization_barrier((summed, odd_rows))
            outputs.append(updated(later))
            three = jnp.stack([rows, even_rows, odd_rows])
            near = spread(three)
            far = send(near, partner_core)
            wholes = []
        else:
            outputs.append(updated(summed))
    return (outputs[-2][None], outputs[-1][None])


def solution(mesh):
    in_specs = (
        P("sec", None, None),
        P("sec", "ops", None, None),
        P("sec", "ops", None, None),
        P("sec", "ops"),
        P(),
    )
    out_specs = (P("sec", "ops", None), P("sec", "ops", None))
    return jax.shard_map(
        on_device, mesh=mesh, in_specs=in_specs, out_specs=out_specs, check_vma=False
    )
```
